32 devices in a mesh: ctx: 2 (over y), row: 8 (over z, x), col: 2 (over core).
Axes of the slice: x: 2, y: 2, z: 4, core: 2. Of those that a mesh axis runs over, the one named last changes fastest.
Arguments:
- context_map: bfloat16 [128, 512, 256], P(('ctx', 'row'), 'col'), parts along dimension 0, may hold values from -6 to 6
- norm_gains: float32 [3, 256], replicated, may hold values from 0.25 to 1.75
- conv_biases: float32 [3, 256], replicated, may hold values from -3 to 3
- conv_weights: bfloat16 [3, 3, 3, 256, 256], replicated, may hold values from -0.125 to 0.125
Outputs:
- refined: bfloat16 [128, 512, 256], P(('ctx', 'row'), 'col'), parts along dimension 0
The draws below stay inside these ranges and needn't reach their ends.
There are 2 independent parts, one for each index of `ctx`. The reference program is written for one: setup_inputs(seed, part) draws one part's arguments, and reference() takes and returns one part's arrays. A program takes and returns all parts, laid end to end along the dimension named above; an argument that names none is the same for every part. Nothing has to cross between parts.
All inputs are finite; a program needn't handle non-finite values.
Results may differ from the reference program's by a relative error of at most 0.0052.
Values may be sent and summed in bfloat16 or wider, within the bound.
A program may use at most 64 MiB of HBM per device.

```python
import jax
import jax.numpy as jnp
from jax import lax

C = 256
H = 64
W = 512


def block_levels(key, dims, shards, low, top_value):
    gain, own = 1.0, jax.random.fold_in(key, 6)
    for axis_at, shards_of in shards:
        heights = jnp.exp(jax.random.uniform(jax.random.fold_in(own, axis_at), (shards_of,), jnp.float32, low / len(shards), top_value / len(shards)))
        gain = gain * jnp.repeat(heights, dims[axis_at] // shards_of).reshape([-1 if axis == axis_at else 1 for axis in range(len(dims))])
    return gain


def gaussian(rng, dims, spread, bound, split=(), dtype=jnp.bfloat16):
    level = block_levels(rng, dims, split, -0.22, 0.18) if split else 1.0
    array = jax.random.normal(rng, dims, jnp.float32) * spread * level
    return jnp.minimum(jnp.maximum(array, -bound), bound).astype(dtype)


def setup_inputs(seed: int = 0, part: int = 0) -> dict:
    key_list = jax.random.split(jax.random.key(seed), 5)
    part_splits = jax.random.split(jax.random.fold_in(key_list[4], part), 5)
    context_map = gaussian(part_splits[0], (H, W, C), 1.0, 6.0, ((0, 8), (1, 2)))
    norm_gains = jnp.clip(1.0 + 0.15 * jax.random.normal(key_list[1], (3, C), jnp.float32), 0.25, 1.75)
    conv_biases = gaussian(key_list[2], (3, C), 0.5, 3.0, (), jnp.float32)
    conv_weights = gaussian(key_list[3], (3, 3, 3, C, C), (9 * C) ** -0.5, 0.125)
    return dict(context_map=context_map, norm_gains=norm_gains, conv_biases=conv_biases, conv_weights=conv_weights)


def one_layer(current, weight, gain_row, bias_row, dilation):
    values = current.astype(jnp.float32)
    centred = values - lax.optimization_barrier(jnp.mean(values, axis=-1, keepdims=True))
    variance = lax.optimization_barrier(jnp.mean(centred * centred, axis=-1, keepdims=True))
    normed = (centred * lax.rsqrt(variance + 1e-05) * gain_row).astype(jnp.bfloat16)
    normed = lax.optimization_barrier(normed)
    response = lax.conv_general_dilated(normed.astype(jnp.float32)[None], weight.astype(jnp.float32), (1, 1), ((dilation, dilation), (dilation, dilation)), rhs_dilation=(dilation, dilation), dimension_numbers=('NHWC', 'HWIO', 'NHWC'), precision=lax.Precision.HIGHEST)[0]
    return (values + jnp.maximum(response + bias_row, 0.0)).astype(jnp.bfloat16)

def reference(context_map, norm_gains, conv_biases, conv_weights):
    current = context_map
    for position, dilation in ((0, 4), (1, 32), (2, 64)):
        current = one_layer(current, conv_weights[position], norm_gains[position], conv_biases[position], dilation)
    return current
```

```python
import functools

import jax
import jax.numpy as jnp
from jax import lax
from jax.experimental import pallas as pl
from jax.experimental.pallas import tpu as pltpu
from jax.sharding import PartitionSpec as P

epsilon = 1e-05
dilations = (4, 32, 64)


def extended(x, sides, width):
    for axis, dim in sides:
        size, length = (lax.axis_size(axis), x.shape[dim])
        up = [(i, (i + 1) % size) for i in range(size - 1)]
        down = [(j, i) for i, j in up]
        last = lax.slice_in_dim(x, length - width, length, axis=dim)
        first = lax.slice_in_dim(x, 0, width, axis=dim)
        before = lax.ppermute(last, axis, up)
        after = lax.ppermute(first, axis, down)
        x = jnp.concatenate([before, x, after], axis=dim)
    return x


def normalize(current, gain_row):
    values = current.astype(jnp.float32)
    centred = values - jnp.mean(values, axis=-1, keepdims=True)
    variance = jnp.mean(centred * centred, axis=-1, keepdims=True)
    return (centred * lax.rsqrt(variance + epsilon) * gain_row).astype(jnp.bfloat16)


def convolve(padded, kernel, row_step, col_step, out_rows, out_cols):
    channels = padded.shape[2]
    tap_list = []
    for tap_row in range(3):
        for tap_col in range(3):
            tap_list.append(
                lax.slice(
                    padded,
                    (tap_row * row_step, tap_col * col_step, 0),
                    (tap_row * row_step + out_rows, tap_col * col_step + out_cols, channels),
                )
            )
    stacked = jnp.concatenate(tap_list, axis=2).reshape(out_rows * out_cols, 9 * channels)
    product = jnp.dot(
        stacked, kernel.reshape(9 * channels, kernel.shape[3]), preferred_element_type=jnp.float32
    )
    return product.reshape(out_rows, out_cols, kernel.shape[3])


def update(current, response, bias_row):
    return (current.astype(jnp.float32) + jnp.maximum(response + bias_row, 0.0)).astype(
        jnp.bfloat16
    )


def class_rims(normed, width):
    return extended(normed, (("col", 1),), width)


def streamed(
    x_hbm, g_ref, b_ref, w_hbm, out_hbm,
    xs, n0, taps, n1, m1, n2, x1, x2, y, w,
    load_sem, w_sem, dn_send, dn_recv, up_send, up_recv, side_send, side_recv,
    swap_send, swap_recv, rim_send, rim_recv, out_sem,
):
    tile_rows, tile_cols, channels = x_hbm.shape
    halo, wide = dilations[0], dilations[1]
    edge = 16
    slots = tile_cols // wide
    cells = tile_rows * wide
    i, n = lax.axis_index("row"), lax.axis_size("row")
    c = lax.axis_index("col")
    other = 1 - c
    above, below = lax.rem(i + n - 1, n), lax.rem(i + 1, n)
    shift = dilations[1] // tile_rows
    partner = lax.rem(i + shift, n)
    partner_tap = jnp.where(i < shift, 2, 0)
    outward = 1 - 2 * c
    has_above, has_below = i > 0, i < n - 1

    def columns(s):
        return pl.ds(
            pl.multiple_of(c * wide * (s - 1) + other * (tile_cols - wide * s), wide), wide
        )

    def remote(src, dst, send, recv, row, col):
        return pltpu.make_async_remote_copy(
            src_ref=src,
            dst_ref=dst,
            send_sem=send,
            recv_sem=recv,
            device_id={"row": row, "col": col},
            device_id_type=pl.DeviceIdType.MESH,
        )

    def load(s):
        return pltpu.make_async_copy(
            x_hbm.at[:, columns(s), :], xs.at[s, halo : halo + tile_rows], load_sem.at[s - 1]
        )

    def load_w(layer):
        return pltpu.make_async_copy(w_hbm.at[layer], w.at[layer], w_sem.at[layer])

    def halo_down(s):
        return remote(
            x_hbm.at[tile_rows - halo :, columns(s), :], xs.at[s, :halo],
            dn_send.at[s - 1], dn_recv.at[s - 1], below, c,
        )

    def halo_up(s):
        return remote(
            x_hbm.at[:halo, columns(s), :], xs.at[s, halo + tile_rows :],
            up_send.at[s - 1], up_recv.at[s - 1], above, c,
        )

    side_from = pl.ds(pl.multiple_of(other * (tile_cols - edge), edge), edge)
    side_to = pl.ds(pl.multiple_of(other * (wide - edge), edge), edge)

    side = remote(
        x_hbm.at[:, side_from, :], xs.at[0, halo : halo + tile_rows, side_to, :],
        side_send.at[0], side_recv.at[0], i, other,
    )
    corner_down = remote(
        x_hbm.at[tile_rows - halo :, side_from, :], xs.at[0, :halo, side_to, :],
        side_send.at[1], side_recv.at[1], below, other,
    )
    corner_up = remote(
        x_hbm.at[:halo, side_from, :], xs.at[0, halo + tile_rows :, side_to, :],
        side_send.at[2], side_recv.at[2], above, other,
    )

    def swap(s):
        return remote(
            n1.at[s], m1.at[s], swap_send.at[s - 1], swap_recv.at[s - 1], partner, c
        )

    rim_own = remote(n1.at[1], n1.at[0], rim_send.at[0], rim_recv.at[0], i, other)
    rim_partner = remote(m1.at[1], m1.at[0], rim_send.at[1], rim_recv.at[1], i, other)
    rim_next = [
        remote(n2.at[1 + s], n2.at[2 - s], rim_send.at[1 + s], rim_recv.at[1 + s], i, other)
        for s in (1, 2)
    ]

    def store(s):
        return pltpu.make_async_copy(
            y.at[s - 1], out_hbm.at[:, columns(s), :], out_sem.at[s - 1]
        )

    def norm(values, layer):
        values = values.astype(jnp.float32)
        centred = values - jnp.mean(values, axis=-1, keepdims=True)
        variance = jnp.mean(centred * centred, axis=-1, keepdims=True)
        gain = g_ref[layer : layer + 1, :].reshape((1,) * (values.ndim - 1) + (channels,))
        return (centred * lax.rsqrt(variance + epsilon) * gain).astype(jnp.bfloat16)

    def residual(values, response, layer):
        return (
            values.reshape(cells, channels).astype(jnp.float32)
            + jnp.maximum(response + b_ref[layer : layer + 1, :], 0.0)
        ).astype(jnp.bfloat16)

    def dot(a, b):
        return jnp.dot(a, b, preferred_element_type=jnp.float32)

    def row_of(ref, s, step):
        return jnp.concatenate(
            [ref[at].reshape(cells, channels) for at in (s + step, s, s - step)], axis=1
        )

    @pl.loop(1, slots + 1)
    def _(s):
        load(s).start()

    for layer in range(3):
        load_w(layer).start()

    barrier = pltpu.get_barrier_semaphore()
    zeros = functools.partial(jnp.zeros, dtype=jnp.bfloat16)
    xs[0] = zeros(xs.shape[1:])

    @pl.when(i == 0)
    def _():
        xs[:, :halo] = zeros((slots + 1, halo, wide, channels))

    @pl.when(i == n - 1)
    def _():
        xs[:, halo + tile_rows :] = zeros((slots + 1, halo, wide, channels))

    def greet(row, col):
        pl.semaphore_signal(
            barrier, inc=1, device_id={"row": row, "col": col},
            device_id_type=pl.DeviceIdType.MESH,
        )

    greet(i, other)
    greet(partner, c)

    @pl.when(has_above)
    def _():
        greet(above, c)
        greet(above, other)

    @pl.when(has_below)
    def _():
        greet(below, c)
        greet(below, other)

    n0[slots + 1] = zeros(n0.shape[1:])
    n1[slots + 1] = zeros(n1.shape[1:])
    m1[slots + 1] = zeros(m1.shape[1:])
    n2[slots + 2] = zeros(n2.shape[1:])
    n2[slots + 3] = zeros(n2.shape[1:])
    pl.semaphore_wait(barrier, 2 + 2 * jnp.minimum(i, 1) + 2 * jnp.minimum(n - 1 - i, 1))

    side.start()

    @pl.when(has_below)
    def _():
        corner_down.start()

    @pl.when(has_above)
    def _():
        corner_up.start()

    @pl.loop(1, slots + 1)
    def _(s):
        @pl.when(has_below)
        def _():
            halo_down(s).start()

        @pl.when(has_above)
        def _():
            halo_up(s).start()

    def arrive(s):
        load(s).wait()

        @pl.when(has_above)
        def _():
            halo_down(s).wait_recv()

        @pl.when(has_below)
        def _():
            halo_up(s).wait_recv()

    def norm_slot(s):
        @pl.loop(0, xs.shape[1] // halo)
        def _(part):
            rows = pl.ds(part * halo, halo)
            n0[s, rows] = norm(xs[s, rows], 0)

    side.wait_recv()

    @pl.when(has_above)
    def _():
        corner_down.wait_recv()

    @pl.when(has_below)
    def _():
        corner_up.wait_recv()

    load_w(0).wait()

    @pl.loop(0, slots + 2)
    def _(s):
        @pl.when((s > 0) & (s <= slots))
        def _():
            arrive(s)

        @pl.when(s <= slots)
        def _():
            norm_slot(s)

        @pl.when(s > 1)
        def _():
            at = s - 1
            left, right = at + outward, at - outward

            @pl.loop(0, xs.shape[1] // halo)
            def _(part):
                rows = pl.ds(part * halo, halo)
                centre = n0[at, rows]
                around = jnp.concatenate(
                    [n0[left, rows, wide - edge :, :], centre, n0[right, rows, :edge, :]], axis=1
                ).astype(jnp.float32)
                span = wide + 2 * edge
                lower = pltpu.roll(around, halo, 1)[:, edge : edge + wide]
                upper = pltpu.roll(around, span - halo, 1)[:, edge : edge + wide]
                taps[rows, :, :channels] = lower.astype(jnp.bfloat16)
                taps[rows, :, channels : 2 * channels] = centre
                taps[rows, :, 2 * channels :] = upper.astype(jnp.bfloat16)

            response = dot(taps[:tile_rows].reshape(cells, 3 * channels), w[0, 0])
            for tap in (1, 2):
                response += dot(
                    taps[tap * halo : tap * halo + tile_rows].reshape(cells, 3 * channels),
                    w[0, tap],
                )
            current = residual(xs[at, halo : halo + tile_rows], response, 0)
            x1[at - 1] = current
            n1[at] = norm(current, 1).reshape(tile_rows, wide, channels)
            swap(at).start()

            @pl.when(at == 1)
            def _():
                rim_own.start()

    load_w(1).wait()
    load_w(2).wait()
    rim_own.wait_recv()
    swap(1).wait_recv()
    rim_partner.start()

    @pl.loop(1, slots + 3)
    def _(s):
        @pl.when(s < slots)
        def _():
            swap(s + 1).wait_recv()

        @pl.when(s == 1)
        def _():
            rim_partner.wait_recv()

        @pl.when(s <= slots)
        def _():
            response = dot(row_of(n1, s, outward), w[1, 1])
            response += dot(row_of(m1, s, outward), w[1, partner_tap])
            current = residual(x1[s - 1].reshape(tile_rows, wide, channels), response, 1)
            x2[s - 1] = current
            n2[s + 1] = norm(current, 2).reshape(tile_rows, wide, channels)

        for k in (1, 2):
            @pl.when(s == k)
            def _():
                rim_next[k - 1].start()

        @pl.when(s == 3)
        def _():
            for copy in rim_next:
                copy.wait_recv()

        @pl.when(s >= 3)
        def _():
            at = s - 2
            response = dot(row_of(n2, at + 1, 2 * outward), w[2, 1])
            current = residual(x2[at - 1].reshape(tile_rows, wide, channels), response, 2)
            y[at - 1] = current.reshape(tile_rows, wide, channels)
            store(at).start()

    side.wait_send()
    rim_own.wait_send()
    rim_partner.wait_send()
    for copy in rim_next:
        copy.wait_send()

    @pl.when(has_below)
    def _():
        corner_down.wait_send()

    @pl.when(has_above)
    def _():
        corner_up.wait_send()

    @pl.loop(1, slots + 1)
    def _(s):
        @pl.when(has_below)
        def _():
            halo_down(s).wait_send()

        @pl.when(has_above)
        def _():
            halo_up(s).wait_send()

        swap(s).wait_send()
        store(s).wait()


def paired(mesh, shape):
    tile_rows, tile_cols, channels = shape
    rows = mesh["row"] * tile_rows
    return (
        mesh["col"] == 2
        and rows == 2 * dilations[1]
        and rows <= dilations[2]
        and dilations[2] == 2 * dilations[1]
        and dilations[1] % tile_rows == 0
        and mesh["row"] > 2
        and tile_rows == 2 * dilations[0]
        and tile_cols % dilations[1] == 0
        and tile_cols >= dilations[2]
        and channels % 128 == 0
    )


def streamed_shards(context_map, norm_gains, conv_biases, conv_weights):
    tile_rows, tile_cols, channels = context_map.shape
    halo, wide = dilations[0], dilations[1]
    slots = tile_cols // wide
    tall = tile_rows + 2 * halo
    bf16 = jnp.bfloat16
    dma = pltpu.SemaphoreType.DMA
    cell = (tile_rows, wide, channels)
    return pl.pallas_call(
        streamed,
        out_shape=jax.ShapeDtypeStruct(context_map.shape, bf16),
        in_specs=[
            pl.BlockSpec(memory_space=pltpu.HBM),
            pl.BlockSpec(memory_space=pltpu.VMEM),
            pl.BlockSpec(memory_space=pltpu.VMEM),
            pl.BlockSpec(memory_space=pltpu.HBM),
        ],
        out_specs=pl.BlockSpec(memory_space=pltpu.HBM),
        scratch_shapes=[
            pltpu.VMEM((slots + 1, tall, wide, channels), bf16),
            pltpu.VMEM((slots + 2, tall, wide, channels), bf16),
            pltpu.VMEM((tall, wide, 3 * channels), bf16),
            pltpu.VMEM((slots + 2,) + cell, bf16),
            pltpu.VMEM((slots + 2,) + cell, bf16),
            pltpu.VMEM((slots + 4,) + cell, bf16),
            pltpu.VMEM((slots, tile_rows * wide, channels), bf16),
            pltpu.VMEM((slots, tile_rows * wide, channels), bf16),
            pltpu.VMEM((slots,) + cell, bf16),
            pltpu.VMEM((3, 3, 3 * channels, channels), bf16),
            dma((slots,)),
            dma((3,)),
            dma((slots,)), dma((slots,)),
            dma((slots,)), dma((slots,)),
            dma((3,)), dma((3,)),
            dma((slots,)), dma((slots,)),
            dma((4,)), dma((4,)),
            dma((slots,)),
        ],
        compiler_params=pltpu.CompilerParams(
            collective_id=0, has_side_effects=True, vmem_limit_bytes=48 * 1024 * 1024
        ),
    )(
        context_map,
        norm_gains,
        conv_biases,
        conv_weights.reshape(3, 3, 3 * channels, channels),
    )


def shards(context_map, norm_gains, conv_biases, conv_weights):
    tile_rows, tile_cols, channels = context_map.shape
    normed = normalize(context_map, norm_gains[0])
    padded = extended(normed, (("row", 0), ("col", 1)), 4)
    current = update(
        context_map, convolve(padded, conv_weights[0], 4, 4, tile_rows, tile_cols), conv_biases[0]
    )
    class_count = lax.axis_size("row") // tile_rows
    sub_cols = tile_cols // class_count
    outgoing = (
        current.reshape(tile_rows, sub_cols, class_count, channels)
        .transpose(0, 2, 1, 3)
        .reshape(tile_rows * class_count, sub_cols, channels)
    )
    grouped = lax.all_to_all(outgoing, "row", split_axis=0, concat_axis=0, tiled=True)
    sub_rows = grouped.shape[0]
    for position, dilation in ((1, 32), (2, 64)):
        normed = normalize(grouped, norm_gains[position])
        row_gap = dilation // tile_rows
        col_gap = dilation // class_count
        with_sides = class_rims(normed, col_gap)
        padded = jnp.pad(with_sides, ((row_gap, row_gap), (0, 0), (0, 0)))
        response = convolve(padded, conv_weights[position], row_gap, col_gap, sub_rows, sub_cols)
        grouped = update(grouped, response, conv_biases[position])
    returned = lax.all_to_all(grouped, "row", split_axis=0, concat_axis=0, tiled=True)
    return (
        returned.reshape(tile_rows, class_count, sub_cols, channels)
        .transpose(0, 2, 1, 3)
        .reshape(tile_rows, tile_cols, channels)
    )


def by_shape(sizes, context_map, *parameters):
    body = streamed_shards if paired(sizes, context_map.shape) else shards
    return body(context_map, *parameters)


def solution(mesh):
    return jax.shard_map(
        functools.partial(by_shape, dict(mesh.shape)),
        mesh=mesh,
        in_specs=(P(("ctx", "row"), "col", None), P(), P(), P()),
        out_specs=P(("ctx", "row"), "col", None),
        check_vma=False,
    )
```

```python
import functools

import jax
import jax.numpy as jnp
from jax import lax
from jax.experimental import pallas as pl
from jax.experimental.pallas import tpu as pltpu
from jax.sharding import PartitionSpec as P

epsilon = 1e-05
dilations = (4, 32, 64)


def extended(x, sides, width):
    for axis, dim in sides:
        size, length = (lax.axis_size(axis), x.shape[dim])
        up = [(i, (i + 1) % size) for i in range(size - 1)]
        down = [(j, i) for i, j in up]
        last = lax.slice_in_dim(x, length - width, length, axis=dim)
        first = lax.slice_in_dim(x, 0, width, axis=dim)
        before = lax.ppermute(last, axis, up)
        after = lax.ppermute(first, axis, down)
        x = jnp.concatenate([before, x, after], axis=dim)
    return x


def normalize(current, gain_row):
    values = current.astype(jnp.float32)
    centred = values - jnp.mean(values, axis=-1, keepdims=True)
    variance = jnp.mean(centred * centred, axis=-1, keepdims=True)
    return (centred * lax.rsqrt(variance + epsilon) * gain_row).astype(jnp.bfloat16)


def convolve(padded, kernel, row_step, col_step, out_rows, out_cols):
    channels = padded.shape[2]
    tap_list = []
    for tap_row in range(3):
        for tap_col in range(3):
            tap_list.append(
                lax.slice(
                    padded,
                    (tap_row * row_step, tap_col * col_step, 0),
                    (tap_row * row_step + out_rows, tap_col * col_step + out_cols, channels),
                )
            )
    stacked = jnp.concatenate(tap_list, axis=2).reshape(out_rows * out_cols, 9 * channels)
    product = jnp.dot(
        stacked, kernel.reshape(9 * channels, kernel.shape[3]), preferred_element_type=jnp.float32
    )
    return product.reshape(out_rows, out_cols, kernel.shape[3])


def update(current, response, bias_row):
    return (current.astype(jnp.float32) + jnp.maximum(response + bias_row, 0.0)).astype(
        jnp.bfloat16
    )


def class_rims(normed, width):
    return extended(normed, (("col", 1),), width)


def streamed(
    x_hbm, g_hbm, b_hbm, w_hbm, out_hbm,
    xs, n0, taps, n1, m1, n2, x1, x2, y, w, g_ref, b_ref,
    load_sem, w_sem, dn_send, dn_recv, up_send, up_recv, side_send, side_recv,
    swap_send, swap_recv, rim_send, rim_recv, out_sem,
):
    tile_rows, tile_cols, channels = x_hbm.shape
    halo, wide = dilations[0], dilations[1]
    edge = 16
    slots = tile_cols // wide
    cells = tile_rows * wide
    i, n = lax.axis_index("row"), lax.axis_size("row")
    c = lax.axis_index("col")
    other = 1 - c
    above, below = lax.rem(i + n - 1, n), lax.rem(i + 1, n)
    shift = dilations[1] // tile_rows
    partner = lax.rem(i + shift, n)
    partner_tap = jnp.where(i < shift, 2, 0)
    outward = 1 - 2 * c
    has_above, has_below = i > 0, i < n - 1

    def columns(s):
        return pl.ds(
            pl.multiple_of(c * wide * (s - 1) + other * (tile_cols - wide * s), wide), wide
        )

    def remote(src, dst, send, recv, row, col):
        return pltpu.make_async_remote_copy(
            src_ref=src,
            dst_ref=dst,
            send_sem=send,
            recv_sem=recv,
            device_id={"row": row, "col": col},
            device_id_type=pl.DeviceIdType.MESH,
        )

    def load(s):
        return pltpu.make_async_copy(
            x_hbm.at[:, columns(s), :], xs.at[s, halo : halo + tile_rows], load_sem.at[s - 1]
        )

    def load_w(layer):
        return pltpu.make_async_copy(w_hbm.at[layer], w.at[layer], w_sem.at[layer])

    def halo_down(s):
        return remote(
            x_hbm.at[tile_rows - halo :, columns(s), :], xs.at[s, :halo],
            dn_send.at[s - 1], dn_recv.at[s - 1], below, c,
        )

    def halo_up(s):
        return remote(
            x_hbm.at[:halo, columns(s), :], xs.at[s, halo + tile_rows :],
            up_send.at[s - 1], up_recv.at[s - 1], above, c,
        )

    side_from = pl.ds(pl.multiple_of(other * (tile_cols - edge), edge), edge)
    side_to = pl.ds(pl.multiple_of(other * (wide - edge), edge), edge)

    side = remote(
        x_hbm.at[:, side_from, :], xs.at[0, halo : halo + tile_rows, side_to, :],
        side_send.at[0], side_recv.at[0], i, other,
    )
    corner_down = remote(
        x_hbm.at[tile_rows - halo :, side_from, :], xs.at[0, :halo, side_to, :],
        side_send.at[1], side_recv.at[1], below, other,
    )
    corner_up = remote(
        x_hbm.at[:halo, side_from, :], xs.at[0, halo + tile_rows :, side_to, :],
        side_send.at[2], side_recv.at[2], above, other,
    )

    def swap(s):
        return remote(
            n1.at[s], m1.at[s], swap_send.at[s - 1], swap_recv.at[s - 1], partner, c
        )

    rim_own = remote(n1.at[1], n1.at[0], rim_send.at[0], rim_recv.at[0], i, other)
    rim_partner = remote(m1.at[1], m1.at[0], rim_send.at[1], rim_recv.at[1], i, other)
    rim_next = [
        remote(n2.at[1 + s], n2.at[2 - s], rim_send.at[1 + s], rim_recv.at[1 + s], i, other)
        for s in (1, 2)
    ]

    def store(s):
        return pltpu.make_async_copy(
            y.at[s - 1], out_hbm.at[:, columns(s), :], out_sem.at[s - 1]
        )

    def norm(values, layer):
        values = values.astype(jnp.float32)
        centred = values - jnp.mean(values, axis=-1, keepdims=True)
        variance = jnp.mean(centred * centred, axis=-1, keepdims=True)
        gain = g_ref[layer : layer + 1, :].reshape((1,) * (values.ndim - 1) + (channels,))
        return (centred * lax.rsqrt(variance + epsilon) * gain).astype(jnp.bfloat16)

    def residual(values, response, layer):
        return (
            values.reshape(cells, channels).astype(jnp.float32)
            + jnp.maximum(response + b_ref[layer : layer + 1, :], 0.0)
        ).astype(jnp.bfloat16)

    def dot(a, b):
        return jnp.dot(a, b, preferred_element_type=jnp.float32)

    def row_of(ref, s, step):
        return jnp.concatenate(
            [ref[at].reshape(cells, channels) for at in (s + step, s, s - step)], axis=1
        )

    @pl.loop(1, slots + 1)
    def _(s):
        load(s).start()

    load_g = pltpu.make_async_copy(g_hbm, g_ref, w_sem.at[3])
    load_b = pltpu.make_async_copy(b_hbm, b_ref, w_sem.at[4])
    load_g.start()
    load_b.start()
    for layer in range(3):
        load_w(layer).start()

    barrier = pltpu.get_barrier_semaphore()
    zeros = functools.partial(jnp.zeros, dtype=jnp.bfloat16)
    xs[0] = zeros(xs.shape[1:])

    @pl.when(i == 0)
    def _():
        xs[:, :halo] = zeros((slots + 1, halo, wide, channels))

    @pl.when(i == n - 1)
    def _():
        xs[:, halo + tile_rows :] = zeros((slots + 1, halo, wide, channels))

    def greet(row, col):
        pl.semaphore_signal(
            barrier, inc=1, device_id={"row": row, "col": col},
            device_id_type=pl.DeviceIdType.MESH,
        )

    greet(i, other)
    greet(partner, c)

    @pl.when(has_above)
    def _():
        greet(above, c)
        greet(above, other)

    @pl.when(has_below)
    def _():
        greet(below, c)
        greet(below, other)

    n0[slots + 1] = zeros(n0.shape[1:])
    n1[slots + 1] = zeros(n1.shape[1:])
    m1[slots + 1] = zeros(m1.shape[1:])
    n2[slots + 2] = zeros(n2.shape[1:])
    n2[slots + 3] = zeros(n2.shape[1:])
    pl.semaphore_wait(barrier, 2 + 2 * jnp.minimum(i, 1) + 2 * jnp.minimum(n - 1 - i, 1))

    side.start()

    @pl.when(has_below)
    def _():
        corner_down.start()

    @pl.when(has_above)
    def _():
        corner_up.start()

    @pl.when(i == shift - 1)
    def _():
        @pl.loop(1, slots + 1)
        def _(s):
            halo_down(s).start()

    @pl.when(i == shift)
    def _():
        @pl.loop(1, slots + 1)
        def _(s):
            halo_up(s).start()

    @pl.loop(1, slots + 1)
    def _(s):
        @pl.when(has_below & (i != shift - 1))
        def _():
            halo_down(s).start()

        @pl.when(has_above & (i != shift))
        def _():
            halo_up(s).start()

    def arrive(s):
        load(s).wait()

        @pl.when(has_above)
        def _():
            halo_down(s).wait_recv()

        @pl.when(has_below)
        def _():
            halo_up(s).wait_recv()

    def norm_slot(s):
        @pl.loop(0, xs.shape[1] // halo)
        def _(part):
            rows = pl.ds(part * halo, halo)
            n0[s, rows] = norm(xs[s, rows], 0)

    side.wait_recv()

    @pl.when(has_above)
    def _():
        corner_down.wait_recv()

    @pl.when(has_below)
    def _():
        corner_up.wait_recv()

    load_g.wait()
    load_b.wait()
    load_w(0).wait()

    @pl.loop(0, slots + 2)
    def _(s):
        @pl.when((s > 0) & (s <= slots))
        def _():
            arrive(s)

        @pl.when(s <= slots)
        def _():
            norm_slot(s)

        @pl.when(s > 1)
        def _():
            at = s - 1
            left, right = at + outward, at - outward

            @pl.loop(0, xs.shape[1] // halo)
            def _(part):
                rows = pl.ds(part * halo, halo)
                centre = n0[at, rows]
                around = jnp.concatenate(
                    [n0[left, rows, wide - edge :, :], centre, n0[right, rows, :edge, :]], axis=1
                ).astype(jnp.float32)
                span = wide + 2 * edge
                lower = pltpu.roll(around, halo, 1)[:, edge : edge + wide]
                upper = pltpu.roll(around, span - halo, 1)[:, edge : edge + wide]
                taps[rows, :, :channels] = lower.astype(jnp.bfloat16)
                taps[rows, :, channels : 2 * channels] = centre
                taps[rows, :, 2 * channels :] = upper.astype(jnp.bfloat16)

            response = dot(taps[:tile_rows].reshape(cells, 3 * channels), w[0, 0])
            for tap in (1, 2):
                response += dot(
                    taps[tap * halo : tap * halo + tile_rows].reshape(cells, 3 * channels),
                    w[0, tap],
                )
            current = residual(xs[at, halo : halo + tile_rows], response, 0)
            x1[at - 1] = current
            n1[at] = norm(current, 1).reshape(tile_rows, wide, channels)
            swap(at).start()

            @pl.when(at == 1)
            def _():
                rim_own.start()

    load_w(1).wait()
    load_w(2).wait()
    rim_own.wait_recv()
    swap(1).wait_recv()
    rim_partner.start()

    @pl.loop(1, slots + 3)
    def _(s):
        @pl.when(s < slots)
        def _():
            swap(s + 1).wait_recv()

        @pl.when(s == 1)
        def _():
            rim_partner.wait_recv()

        @pl.when(s <= slots)
        def _():
            response = dot(row_of(n1, s, outward), w[1, 1])
            response += dot(row_of(m1, s, outward), w[1, partner_tap])
            current = residual(x1[s - 1].reshape(tile_rows, wide, channels), response, 1)
            x2[s - 1] = current
            n2[s + 1] = norm(current, 2).reshape(tile_rows, wide, channels)

        for k in (1, 2):
            @pl.when(s == k)
            def _():
                rim_next[k - 1].start()

        @pl.when(s == 3)
        def _():
            for copy in rim_next:
                copy.wait_recv()

        @pl.when(s >= 3)
        def _():
            at = s - 2
            response = dot(row_of(n2, at + 1, 2 * outward), w[2, 1])
            current = residual(x2[at - 1].reshape(tile_rows, wide, channels), response, 2)
            y[at - 1] = current.reshape(tile_rows, wide, channels)
            store(at).start()

    side.wait_send()
    rim_own.wait_send()
    rim_partner.wait_send()
    for copy in rim_next:
        copy.wait_send()

    @pl.when(has_below)
    def _():
        corner_down.wait_send()

    @pl.when(has_above)
    def _():
        corner_up.wait_send()

    @pl.loop(1, slots + 1)
    def _(s):
        @pl.when(has_below)
        def _():
            halo_down(s).wait_send()

        @pl.when(has_above)
        def _():
            halo_up(s).wait_send()

        swap(s).wait_send()
        store(s).wait()


def paired(mesh, shape):
    tile_rows, tile_cols, channels = shape
    rows = mesh["row"] * tile_rows
    return (
        mesh["col"] == 2
        and rows == 2 * dilations[1]
        and rows <= dilations[2]
        and dilations[2] == 2 * dilations[1]
        and dilations[1] % tile_rows == 0
        and mesh["row"] > 2
        and tile_rows == 2 * dilations[0]
        and tile_cols % dilations[1] == 0
        and tile_cols >= dilations[2]
        and channels % 128 == 0
    )


def streamed_shards(context_map, norm_gains, conv_biases, conv_weights):
    tile_rows, tile_cols, channels = context_map.shape
    halo, wide = dilations[0], dilations[1]
    slots = tile_cols // wide
    tall = tile_rows + 2 * halo
    bf16 = jnp.bfloat16
    dma = pltpu.SemaphoreType.DMA
    cell = (tile_rows, wide, channels)
    return pl.pallas_call(
        streamed,
        out_shape=jax.ShapeDtypeStruct(context_map.shape, bf16),
        in_specs=[
            pl.BlockSpec(memory_space=pltpu.HBM),
            pl.BlockSpec(memory_space=pltpu.HBM),
            pl.BlockSpec(memory_space=pltpu.HBM),
            pl.BlockSpec(memory_space=pltpu.HBM),
        ],
        out_specs=pl.BlockSpec(memory_space=pltpu.HBM),
        scratch_shapes=[
            pltpu.VMEM((slots + 1, tall, wide, channels), bf16),
            pltpu.VMEM((slots + 2, tall, wide, channels), bf16),
            pltpu.VMEM((tall, wide, 3 * channels), bf16),
            pltpu.VMEM((slots + 2,) + cell, bf16),
            pltpu.VMEM((slots + 2,) + cell, bf16),
            pltpu.VMEM((slots + 4,) + cell, bf16),
            pltpu.VMEM((slots, tile_rows * wide, channels), bf16),
            pltpu.VMEM((slots, tile_rows * wide, channels), bf16),
            pltpu.VMEM((slots,) + cell, bf16),
            pltpu.VMEM((3, 3, 3 * channels, channels), bf16),
            pltpu.VMEM((3, channels), jnp.float32),
            pltpu.VMEM((3, channels), jnp.float32),
            dma((slots,)),
            dma((5,)),
            dma((slots,)), dma((slots,)),
            dma((slots,)), dma((slots,)),
            dma((3,)), dma((3,)),
            dma((slots,)), dma((slots,)),
            dma((4,)), dma((4,)),
            dma((slots,)),
        ],
        compiler_params=pltpu.CompilerParams(
            collective_id=0, has_side_effects=True, vmem_limit_bytes=67043328
        ),
    )(
        context_map,
        norm_gains,
        conv_biases,
        conv_weights.reshape(3, 3, 3 * channels, channels),
    )


def shards(context_map, norm_gains, conv_biases, conv_weights):
    tile_rows, tile_cols, channels = context_map.shape
    normed = normalize(context_map, norm_gains[0])
    padded = extended(normed, (("row", 0), ("col", 1)), 4)
    current = update(
        context_map, convolve(padded, conv_weights[0], 4, 4, tile_rows, tile_cols), conv_biases[0]
    )
    class_count = lax.axis_size("row") // tile_rows
    sub_cols = tile_cols // class_count
    outgoing = (
        current.reshape(tile_rows, sub_cols, class_count, channels)
        .transpose(0, 2, 1, 3)
        .reshape(tile_rows * class_count, sub_cols, channels)
    )
    grouped = lax.all_to_all(outgoing, "row", split_axis=0, concat_axis=0, tiled=True)
    sub_rows = grouped.shape[0]
    for position, dilation in ((1, 32), (2, 64)):
        normed = normalize(grouped, norm_gains[position])
        row_gap = dilation // tile_rows
        col_gap = dilation // class_count
        with_sides = class_rims(normed, col_gap)
        padded = jnp.pad(with_sides, ((row_gap, row_gap), (0, 0), (0, 0)))
        response = convolve(padded, conv_weights[position], row_gap, col_gap, sub_rows, sub_cols)
        grouped = update(grouped, response, conv_biases[position])
    returned = lax.all_to_all(grouped, "row", split_axis=0, concat_axis=0, tiled=True)
    return (
        returned.reshape(tile_rows, class_count, sub_cols, channels)
        .transpose(0, 2, 1, 3)
        .reshape(tile_rows, tile_cols, channels)
    )


def by_shape(sizes, context_map, *parameters):
    body = streamed_shards if paired(sizes, context_map.shape) else shards
    return body(context_map, *parameters)


def solution(mesh):
    return jax.shard_map(
        functools.partial(by_shape, dict(mesh.shape)),
        mesh=mesh,
        in_specs=(P(("ctx", "row"), "col", None), P(), P(), P()),
        out_specs=P(("ctx", "row"), "col", None),
        check_vma=False,
    )
```

```python
import functools

import jax
import jax.numpy as jnp
from jax import lax
from jax.experimental import pallas as pl
from jax.experimental.pallas import tpu as pltpu
from jax.sharding import PartitionSpec as P

epsilon = 1e-05
dilations = (4, 32, 64)


def extended(x, sides, width):
    for axis, dim in sides:
        size, length = (lax.axis_size(axis), x.shape[dim])
        up = [(i, (i + 1) % size) for i in range(size - 1)]
        down = [(j, i) for i, j in up]
        last = lax.slice_in_dim(x, length - width, length, axis=dim)
        first = lax.slice_in_dim(x, 0, width, axis=dim)
        before = lax.ppermute(last, axis, up)
        after = lax.ppermute(first, axis, down)
        x = jnp.concatenate([before, x, after], axis=dim)
    return x


def normalize(current, gain_row):
    values = current.astype(jnp.float32)
    centred = values - jnp.mean(values, axis=-1, keepdims=True)
    variance = jnp.mean(centred * centred, axis=-1, keepdims=True)
    return (centred * lax.rsqrt(variance + epsilon) * gain_row).astype(jnp.bfloat16)


def convolve(padded, kernel, row_step, col_step, out_rows, out_cols):
    channels = padded.shape[2]
    tap_list = []
    for tap_row in range(3):
        for tap_col in range(3):
            tap_list.append(
                lax.slice(
                    padded,
                    (tap_row * row_step, tap_col * col_step, 0),
                    (tap_row * row_step + out_rows, tap_col * col_step + out_cols, channels),
                )
            )
    stacked = jnp.concatenate(tap_list, axis=2).reshape(out_rows * out_cols, 9 * channels)
    product = jnp.dot(
        stacked, kernel.reshape(9 * channels, kernel.shape[3]), preferred_element_type=jnp.float32
    )
    return product.reshape(out_rows, out_cols, kernel.shape[3])


def update(current, response, bias_row):
    return (current.astype(jnp.float32) + jnp.maximum(response + bias_row, 0.0)).astype(
        jnp.bfloat16
    )


def class_rims(normed, width):
    return extended(normed, (("col", 1),), width)


def streamed(
    x_hbm, g_hbm, b_hbm, w_hbm, out_ref,
    xs, n0, taps, n1, m1, n2, x1, x2, relayed, w, g_ref, b_ref,
    load_sem, w_sem, dn_send, dn_recv, up_send, up_recv, side_send, side_recv,
    swap_send, swap_recv, rim_send, rim_recv, relay_send, relay_recv,
):
    tile_rows, tile_cols, channels = x_hbm.shape
    halo, wide = dilations[0], dilations[1]
    edge = 16
    slots = tile_cols // wide
    cells = tile_rows * wide
    i, n = lax.axis_index("row"), lax.axis_size("row")
    c = lax.axis_index("col")
    other = 1 - c
    above, below = lax.rem(i + n - 1, n), lax.rem(i + 1, n)
    shift = dilations[1] // tile_rows
    partner = lax.rem(i + shift, n)
    partner_tap = jnp.where(i < shift, 2, 0)
    outward = 1 - 2 * c
    has_above, has_below = i > 0, i < n - 1

    def columns(s):
        return pl.ds(
            pl.multiple_of(c * wide * (s - 1) + other * (tile_cols - wide * s), wide), wide
        )

    def remote(src, dst, send, recv, row, col):
        return pltpu.make_async_remote_copy(
            src_ref=src,
            dst_ref=dst,
            send_sem=send,
            recv_sem=recv,
            device_id={"row": row, "col": col},
            device_id_type=pl.DeviceIdType.MESH,
        )

    def load(s):
        return pltpu.make_async_copy(
            x_hbm.at[:, columns(s), :], xs.at[s, halo : halo + tile_rows], load_sem.at[s - 1]
        )

    def load_w(layer):
        return pltpu.make_async_copy(w_hbm.at[layer], w.at[layer], w_sem.at[layer])

    def halo_down(s):
        return remote(
            x_hbm.at[tile_rows - halo :, columns(s), :], xs.at[s, :halo],
            dn_send.at[s - 1], dn_recv.at[s - 1], below, c,
        )

    def halo_up(s):
        return remote(
            x_hbm.at[:halo, columns(s), :], xs.at[s, halo + tile_rows :],
            up_send.at[s - 1], up_recv.at[s - 1], above, c,
        )

    side_from = pl.ds(pl.multiple_of(other * (tile_cols - edge), edge), edge)
    side_to = pl.ds(pl.multiple_of(other * (wide - edge), edge), edge)

    side = remote(
        x_hbm.at[:, side_from, :], xs.at[0, halo : halo + tile_rows, side_to, :],
        side_send.at[0], side_recv.at[0], i, other,
    )
    corner_down = remote(
        x_hbm.at[tile_rows - halo :, side_from, :], xs.at[0, :halo, side_to, :],
        side_send.at[1], side_recv.at[1], below, other,
    )
    corner_up = remote(
        x_hbm.at[:halo, side_from, :], xs.at[0, halo + tile_rows :, side_to, :],
        side_send.at[2], side_recv.at[2], above, other,
    )

    def swap(s):
        return remote(
            n1.at[s], m1.at[s], swap_send.at[s - 1], swap_recv.at[s - 1], partner, c
        )

    rim_own = remote(n1.at[1], n1.at[0], rim_send.at[0], rim_recv.at[0], i, other)
    rim_partner = remote(m1.at[1], m1.at[0], rim_send.at[1], rim_recv.at[1], i, other)
    rim_next = [
        remote(n2.at[1 + s], n2.at[2 - s], rim_send.at[1 + s], rim_recv.at[1 + s], i, other)
        for s in (1, 2)
    ]

    before, after = shift - 2, shift + 1
    near_middle = (i >= before) & (i <= after)
    across = jnp.where(i < shift, lax.rem(i + 2, n), lax.rem(i + n - 2, n))

    def relay_row(s):
        return jnp.where(lax.rem(s, 2) == 1, before, after)

    def relay_down(s):
        return remote(
            x_hbm.at[tile_rows - halo :, columns(s), :], relayed.at[0, s - 1],
            dn_send.at[s - 1], relay_recv.at[0, s - 1], relay_row(s), c,
        )

    def relay_up(s):
        return remote(
            x_hbm.at[:halo, columns(s), :], relayed.at[1, s - 1],
            up_send.at[s - 1], relay_recv.at[1, s - 1], relay_row(s), c,
        )

    def forward_down(s):
        return remote(
            relayed.at[0, s - 1], xs.at[s, :halo],
            relay_send.at[0, s - 1], dn_recv.at[s - 1], shift, c,
        )

    def forward_up(s):
        return remote(
            relayed.at[1, s - 1], xs.at[s, halo + tile_rows :],
            relay_send.at[1, s - 1], up_recv.at[s - 1], shift - 1, c,
        )

    def relay(s):
        relay_down(s).wait_recv()
        forward_down(s).start()
        relay_up(s).wait_recv()
        forward_up(s).start()

    def norm(values, layer):
        values = values.astype(jnp.float32)
        centred = values - jnp.mean(values, axis=-1, keepdims=True)
        variance = jnp.mean(centred * centred, axis=-1, keepdims=True)
        gain = g_ref[layer : layer + 1, :].reshape((1,) * (values.ndim - 1) + (channels,))
        return (centred * lax.rsqrt(variance + epsilon) * gain).astype(jnp.bfloat16)

    def residual(values, response, layer):
        return (
            values.reshape(cells, channels).astype(jnp.float32)
            + jnp.maximum(response + b_ref[layer : layer + 1, :], 0.0)
        ).astype(jnp.bfloat16)

    def dot(a, b):
        return jnp.dot(a, b, preferred_element_type=jnp.float32)

    def row_of(ref, s, step):
        return jnp.concatenate(
            [ref[at].reshape(cells, channels) for at in (s + step, s, s - step)], axis=1
        )

    @pl.loop(1, slots + 1)
    def _(s):
        load(s).start()

    load_g = pltpu.make_async_copy(g_hbm, g_ref, w_sem.at[3])
    load_b = pltpu.make_async_copy(b_hbm, b_ref, w_sem.at[4])
    load_g.start()
    load_b.start()
    for layer in range(3):
        load_w(layer).start()

    barrier = pltpu.get_barrier_semaphore()
    zeros = functools.partial(jnp.zeros, dtype=jnp.bfloat16)
    xs[0] = zeros(xs.shape[1:])

    @pl.when(i == 0)
    def _():
        xs[:, :halo] = zeros((slots + 1, halo, wide, channels))

    @pl.when(i == n - 1)
    def _():
        xs[:, halo + tile_rows :] = zeros((slots + 1, halo, wide, channels))

    def greet(row, col):
        pl.semaphore_signal(
            barrier, inc=1, device_id={"row": row, "col": col},
            device_id_type=pl.DeviceIdType.MESH,
        )

    greet(i, other)
    greet(partner, c)

    @pl.when(has_above)
    def _():
        greet(above, c)
        greet(above, other)

    @pl.when(has_below)
    def _():
        greet(below, c)
        greet(below, other)

    @pl.when(near_middle)
    def _():
        greet(across, c)

    n0[slots + 1] = zeros(n0.shape[1:])
    n1[slots + 1] = zeros(n1.shape[1:])
    m1[slots + 1] = zeros(m1.shape[1:])
    n2[slots + 2] = zeros(n2.shape[1:])
    n2[slots + 3] = zeros(n2.shape[1:])
    pl.semaphore_wait(barrier, 2 + 2 * jnp.minimum(i, 1) + 2 * jnp.minimum(n - 1 - i, 1) + near_middle.astype(jnp.int32))

    side.start()

    @pl.when(has_below)
    def _():
        corner_down.start()

    @pl.when(has_above)
    def _():
        corner_up.start()

    @pl.loop(1, slots + 1)
    def _(s):
        @pl.when(i == shift - 1)
        def _():
            relay_down(s).start()

        @pl.when(i == shift)
        def _():
            relay_up(s).start()

        @pl.when(has_below & (i != shift - 1))
        def _():
            halo_down(s).start()

        @pl.when(has_above & (i != shift))
        def _():
            halo_up(s).start()

    def arrive(s):
        load(s).wait()

        @pl.when(has_above)
        def _():
            halo_down(s).wait_recv()

        @pl.when(has_below)
        def _():
            halo_up(s).wait_recv()

    def norm_slot(s):
        @pl.loop(0, xs.shape[1] // halo)
        def _(part):
            rows = pl.ds(part * halo, halo)
            n0[s, rows] = norm(xs[s, rows], 0)

    side.wait_recv()

    @pl.when(has_above)
    def _():
        corner_down.wait_recv()

    @pl.when(has_below)
    def _():
        corner_up.wait_recv()

    load_g.wait()
    load_b.wait()
    load_w(0).wait()

    @pl.loop(0, slots + 2)
    def _(s):
        @pl.when((i == before) & (s < slots // 2))
        def _():
            relay(2 * s + 1)

        @pl.when((i == after) & (s < slots // 2))
        def _():
            relay(2 * s + 2)

        @pl.when((s > 0) & (s <= slots))
        def _():
            arrive(s)

        @pl.when(s <= slots)
        def _():
            norm_slot(s)

        @pl.when(s > 1)
        def _():
            at = s - 1
            left, right = at + outward, at - outward

            @pl.loop(0, xs.shape[1] // halo)
            def _(part):
                rows = pl.ds(part * halo, halo)
                centre = n0[at, rows]
                around = jnp.concatenate(
                    [n0[left, rows, wide - edge :, :], centre, n0[right, rows, :edge, :]], axis=1
                ).astype(jnp.float32)
                span = wide + 2 * edge
                lower = pltpu.roll(around, halo, 1)[:, edge : edge + wide]
                upper = pltpu.roll(around, span - halo, 1)[:, edge : edge + wide]
                taps[rows, :, :channels] = lower.astype(jnp.bfloat16)
                taps[rows, :, channels : 2 * channels] = centre
                taps[rows, :, 2 * channels :] = upper.astype(jnp.bfloat16)

            response = dot(taps[:tile_rows].reshape(cells, 3 * channels), w[0, 0])
            for tap in (1, 2):
                response += dot(
                    taps[tap * halo : tap * halo + tile_rows].reshape(cells, 3 * channels),
                    w[0, tap],
                )
            current = residual(xs[at, halo : halo + tile_rows], response, 0)
            x1[at - 1] = current
            n1[at] = norm(current, 1).reshape(tile_rows, wide, channels)
            swap(at).start()

            @pl.when(at == 1)
            def _():
                rim_own.start()

    load_w(1).wait()
    load_w(2).wait()
    rim_own.wait_recv()
    swap(1).wait_recv()
    rim_partner.start()

    @pl.loop(1, slots + 3)
    def _(s):
        @pl.when(s < slots)
        def _():
            swap(s + 1).wait_recv()

        @pl.when(s == 1)
        def _():
            rim_partner.wait_recv()

        @pl.when(s <= slots)
        def _():
            response = dot(row_of(n1, s, outward), w[1, 1])
            response += dot(row_of(m1, s, outward), w[1, partner_tap])
            current = residual(x1[s - 1].reshape(tile_rows, wide, channels), response, 1)
            x2[s - 1] = current
            n2[s + 1] = norm(current, 2).reshape(tile_rows, wide, channels)

        for k in (1, 2):
            @pl.when(s == k)
            def _():
                rim_next[k - 1].start()

        @pl.when(s == 3)
        def _():
            for copy in rim_next:
                copy.wait_recv()

        @pl.when(s >= 3)
        def _():
            at = s - 2
            response = dot(row_of(n2, at + 1, 2 * outward), w[2, 1])
            current = residual(x2[at - 1].reshape(tile_rows, wide, channels), response, 2)
            out_ref[:, columns(at), :] = current.reshape(tile_rows, wide, channels)

    side.wait_send()
    rim_own.wait_send()
    rim_partner.wait_send()
    for copy in rim_next:
        copy.wait_send()

    @pl.when(has_below)
    def _():
        corner_down.wait_send()

    @pl.when(has_above)
    def _():
        corner_up.wait_send()

    @pl.loop(1, slots + 1)
    def _(s):
        @pl.when(has_below)
        def _():
            halo_down(s).wait_send()

        @pl.when(has_above)
        def _():
            halo_up(s).wait_send()

        swap(s).wait_send()

    @pl.loop(0, slots // 2)
    def _(k):
        for row, s in ((before, 2 * k + 1), (after, 2 * k + 2)):
            @pl.when(i == row)
            def _():
                forward_down(s).wait_send()
                forward_up(s).wait_send()


def paired(mesh, shape):
    tile_rows, tile_cols, channels = shape
    rows = mesh["row"] * tile_rows
    return (
        mesh["col"] == 2
        and rows == 2 * dilations[1]
        and rows <= dilations[2]
        and dilations[2] == 2 * dilations[1]
        and dilations[1] % tile_rows == 0
        and mesh["row"] > 2
        and tile_cols % (2 * dilations[1]) == 0
        and tile_rows == 2 * dilations[0]
        and tile_cols % dilations[1] == 0
        and tile_cols >= dilations[2]
        and channels % 128 == 0
    )


def streamed_shards(context_map, norm_gains, conv_biases, conv_weights):
    tile_rows, tile_cols, channels = context_map.shape
    halo, wide = dilations[0], dilations[1]
    slots = tile_cols // wide
    tall = tile_rows + 2 * halo
    bf16 = jnp.bfloat16
    dma = pltpu.SemaphoreType.DMA
    cell = (tile_rows, wide, channels)
    return pl.pallas_call(
        streamed,
        out_shape=jax.ShapeDtypeStruct(context_map.shape, bf16),
        in_specs=[
            pl.BlockSpec(memory_space=pltpu.HBM),
            pl.BlockSpec(memory_space=pltpu.HBM),
            pl.BlockSpec(memory_space=pltpu.HBM),
            pl.BlockSpec(memory_space=pltpu.HBM),
        ],
        out_specs=pl.BlockSpec(memory_space=pltpu.VMEM),
        scratch_shapes=[
            pltpu.VMEM((slots + 1, tall, wide, channels), bf16),
            pltpu.VMEM((slots + 2, tall, wide, channels), bf16),
            pltpu.VMEM((tall, wide, 3 * channels), bf16),
            pltpu.VMEM((slots + 2,) + cell, bf16),
            pltpu.VMEM((slots + 2,) + cell, bf16),
            pltpu.VMEM((slots + 4,) + cell, bf16),
            pltpu.VMEM((slots, tile_rows * wide, channels), bf16),
            pltpu.VMEM((slots, tile_rows * wide, channels), bf16),
            pltpu.VMEM((2, slots, halo, wide, channels), bf16),
            pltpu.VMEM((3, 3, 3 * channels, channels), bf16),
            pltpu.VMEM((3, channels), jnp.float32),
            pltpu.VMEM((3, channels), jnp.float32),
            dma((slots,)),
            dma((5,)),
            dma((slots,)), dma((slots,)),
            dma((slots,)), dma((slots,)),
            dma((3,)), dma((3,)),
            dma((slots,)), dma((slots,)),
            dma((4,)), dma((4,)),
            dma((2, slots)), dma((2, slots)),
        ],
        compiler_params=pltpu.CompilerParams(
            collective_id=0, has_side_effects=True, vmem_limit_bytes=67043328
        ),
    )(
        context_map,
        norm_gains,
        conv_biases,
        conv_weights.reshape(3, 3, 3 * channels, channels),
    )


def shards(context_map, norm_gains, conv_biases, conv_weights):
    tile_rows, tile_cols, channels = context_map.shape
    normed = normalize(context_map, norm_gains[0])
    padded = extended(normed, (("row", 0), ("col", 1)), 4)
    current = update(
        context_map, convolve(padded, conv_weights[0], 4, 4, tile_rows, tile_cols), conv_biases[0]
    )
    class_count = lax.axis_size("row") // tile_rows
    sub_cols = tile_cols // class_count
    outgoing = (
        current.reshape(tile_rows, sub_cols, class_count, channels)
        .transpose(0, 2, 1, 3)
        .reshape(tile_rows * class_count, sub_cols, channels)
    )
    grouped = lax.all_to_all(outgoing, "row", split_axis=0, concat_axis=0, tiled=True)
    sub_rows = grouped.shape[0]
    for position, dilation in ((1, 32), (2, 64)):
        normed = normalize(grouped, norm_gains[position])
        row_gap = dilation // tile_rows
        col_gap = dilation // class_count
        with_sides = class_rims(normed, col_gap)
        padded = jnp.pad(with_sides, ((row_gap, row_gap), (0, 0), (0, 0)))
        response = convolve(padded, conv_weights[position], row_gap, col_gap, sub_rows, sub_cols)
        grouped = update(grouped, response, conv_biases[position])
    returned = lax.all_to_all(grouped, "row", split_axis=0, concat_axis=0, tiled=True)
    return (
        returned.reshape(tile_rows, class_count, sub_cols, channels)
        .transpose(0, 2, 1, 3)
        .reshape(tile_rows, tile_cols, channels)
    )


def by_shape(sizes, context_map, *parameters):
    body = streamed_shards if paired(sizes, context_map.shape) else shards
    return body(context_map, *parameters)


def solution(mesh):
    return jax.shard_map(
        functools.partial(by_shape, dict(mesh.shape)),
        mesh=mesh,
        in_specs=(P(("ctx", "row"), "col", None), P(), P(), P()),
        out_specs=P(("ctx", "row"), "col", None),
        check_vma=False,
    )
```
